32 devices in a mesh: col: 2 (over core), dev: 16 (over z, y, x).
Axes of the slice: x: 2, y: 2, z: 4, core: 2. Of those that a mesh axis runs over, the one named last changes fastest.
Arguments:
- factor_a: float32 [1536, 16, 512], P('dev'), may hold values from -1 to 1
- factor_b: float32 [1536, 64, 512], P('dev', 'col'), may hold values from -1 to 1
- factor_occ: float32 [1536, 16, 512], P('dev'), may hold values from -1 to 1
- singles_a: float32 [16, 16], replicated, may hold values from -1.5 to 1.5
- singles_b: float32 [16, 64], P(None, 'col'), may hold values from -1.5 to 1.5
- doubles: bfloat16 [512, 512, 256], P('col', 'dev'), may hold values from -0.023925781 to 0.023925781
- orbital_a: float32 [16], P('col'), may hold values from 0.2 to 3
- orbital_b: float32 [64], P('dev'), may hold values from 0.2 to 3
- orbital_occ: float32 [16], replicated, may hold values from -2 to -0.3
Outputs:
- update: float32 [16, 64, 256], P('col', 'dev')
The draws below stay inside these ranges and needn't reach their ends.
All inputs are finite; a program needn't handle non-finite values.
Results may differ from the reference program's by a relative error of at most 0.0049.
Values may be sent and summed in bfloat16 or wider, within the bound.
No kernel may reach another device: no remote copies, remote signals or barrier semaphores. Data moves between devices by JAX's collectives and lax.ppermute only.
A program may use at most 128 MiB of HBM per device.

```python
import jax
import jax.numpy as jnp
from jax import lax

V = 512
NAUX = 1536
O = 16
A = 16
B = 64
PAIRS = 256


def block_scale(own_key, dims, pieces, smallest, top_value):
    level, own = 1.0, jax.random.fold_in(own_key, 6)
    for position, parts in pieces:
        draws = jnp.exp(jax.random.uniform(jax.random.fold_in(own, position), (parts,), jnp.float32, smallest / len(pieces), top_value / len(pieces)))
        level = level * jnp.repeat(draws, dims[position] // parts).reshape([-1 if axis == position else 1 for axis in range(len(dims))])
    return level


def noise(stream_key, shape, scale, bound, pieces=(), held_as=jnp.bfloat16):
    drawn = scale * jax.random.normal(stream_key, shape, jnp.float32)
    if pieces:
        drawn = drawn * block_scale(stream_key, shape, pieces, -0.22, 0.18)
    return jnp.clip(drawn, -bound, bound).astype(held_as)


def setup_inputs(seed: int = 0) -> dict:
    arg_keys = jax.random.split(jax.random.key(seed), 10)
    return {
        "factor_a": noise(arg_keys[0], (NAUX, A, V), 0.16, 1.0, ((0, 16),), jnp.float32),
        "factor_b": noise(arg_keys[1], (NAUX, B, V), 0.16, 1.0, ((0, 16), (1, 2)), jnp.float32),
        "factor_occ": noise(arg_keys[2], (NAUX, O, V), 0.16, 1.0, ((0, 16),), jnp.float32),
        "singles_a": noise(arg_keys[3], (O, A), 0.25, 1.5, (), jnp.float32),
        "singles_b": noise(arg_keys[4], (O, B), 0.25, 1.5, ((1, 2),), jnp.float32),
        "doubles": noise(arg_keys[5], (V, V, PAIRS), 0.004, 0.023925781, ((0, 2), (1, 16))),
        "orbital_a": jnp.clip(0.2 + 2.8 * jax.random.uniform(arg_keys[6], (A,), jnp.float32) ** block_scale(arg_keys[6], (A,), ((0, 2),), -0.2, 0.2), 0.2, 3.0),
        "orbital_b": jnp.clip(0.2 + 2.8 * jax.random.uniform(arg_keys[7], (B,), jnp.float32) ** block_scale(arg_keys[7], (B,), ((0, 16),), -0.2, 0.2), 0.2, 3.0),
        "orbital_occ": jnp.clip(jax.random.uniform(arg_keys[8], (O,), jnp.float32, -2.0, -0.3), -2.0, -0.3),
    }


def reference(factor_a, factor_b, factor_occ, singles_a, singles_b, doubles, orbital_a, orbital_b, orbital_occ):
    highest = lax.Precision.HIGHEST
    dressed_a = (factor_a - jnp.einsum("ka,qkc->qac", singles_a, factor_occ, precision=highest)).astype(jnp.bfloat16)
    dressed_b = (factor_b - jnp.einsum("kb,qkd->qbd", singles_b, factor_occ, precision=highest)).astype(jnp.bfloat16)
    wide_b = dressed_b.astype(jnp.float32)
    amplitude = doubles.astype(jnp.float32)

    def one_row(row_a):
        integral = jnp.einsum("qc,qbd->cbd", row_a.astype(jnp.float32), wide_b, precision=highest)
        integral = lax.optimization_barrier(integral.astype(jnp.bfloat16)).astype(jnp.float32)
        return jnp.einsum("cbd,cdp->bp", integral, amplitude, precision=highest)

    residual = lax.map(one_row, jnp.transpose(dressed_a, (1, 0, 2)))
    pair_energy = (orbital_occ[:, None] + orbital_occ[None, :]).reshape(-1)
    denominator = orbital_a[:, None, None] + orbital_b[None, :, None] - pair_energy[None, None, :]
    return residual / denominator
```

```python
import functools

import jax
import jax.numpy as jnp
from jax import lax
from jax.experimental import pallas as pl
from jax.experimental.pallas import tpu as pltpu
from jax.sharding import PartitionSpec as P

F32 = jnp.float32
BF16 = jnp.bfloat16
LANES = 128
GROUP = 4
CHAIN = 4


def params(n):
    return pltpu.CompilerParams(
        dimension_semantics=("arbitrary",) * n, vmem_limit_bytes=60 * 1024 * 1024
    )


def swap_kernel(t_ref, o_ref, wide):
    c_rows, d_rows, pairs = t_ref.shape
    for part in range(pairs // LANES):
        lanes = slice(part * LANES, (part + 1) * LANES)
        wide[...] = t_ref[:, :, lanes].astype(F32).reshape(c_rows * d_rows, LANES)
        for d in range(d_rows):
            o_ref[d, :, lanes] = wide[pl.ds(d, c_rows, stride=d_rows), :].astype(BF16)


def swap_doubles(doubles):
    c_tile, d_tile, pairs = doubles.shape
    rows = 32
    return pl.pallas_call(
        swap_kernel,
        out_shape=jax.ShapeDtypeStruct((d_tile, c_tile, pairs), BF16),
        grid=(c_tile // rows,),
        in_specs=[pl.BlockSpec((rows, d_tile, pairs), lambda i: (i, 0, 0))],
        out_specs=pl.BlockSpec((d_tile, rows, pairs), lambda i: (0, i, 0)),
        scratch_shapes=[pltpu.VMEM((rows * d_tile, LANES), F32)],
        compiler_params=params(1),
        cost_estimate=pl.CostEstimate(
            flops=0, bytes_accessed=4 * doubles.size, transcendentals=0
        ),
    )(doubles)


def tables(singles):
    occ, rows = singles.shape
    return jnp.broadcast_to(singles.T[:, :, None], (rows, occ, LANES)).reshape(rows * occ, LANES)


def dress_a_kernel(parts, where, *refs):
    f_refs, occ_refs, tab_ref, outs = refs[:parts], refs[parts : 2 * parts], refs[2 * parts], refs[2 * parts + 1 :]
    q_rows = outs[0].shape[0]
    a_rows = f_refs[0].shape[0] // q_rows
    occ_rows = occ_refs[0].shape[0] // q_rows
    width = parts * LANES
    per_out = outs[0].shape[1] // width
    for part in range(parts):
        occ = [occ_refs[part][pl.ds(k, q_rows, stride=occ_rows), :] for k in range(occ_rows)]
        for a in range(a_rows):
            source = lax.rem(a + where[1], a_rows)
            value = f_refs[part][pl.ds(source, q_rows, stride=a_rows), :]
            for k in range(occ_rows):
                value = value - tab_ref[pl.ds(source * occ_rows + k, 1), :] * occ[k]
            start = (a % per_out) * width + part * LANES
            outs[a // per_out][:, start : start + LANES] = value.astype(BF16)


def dress_a(where, factor_a, factor_occ, singles_a, c_tile, chunks):
    shard, a_rows, wide = factor_a.shape
    occ_rows = factor_occ.shape[1]
    q_rows = 16
    parts = c_tile // LANES
    out = jax.ShapeDtypeStruct((shard, a_rows * c_tile // chunks), BF16)

    def windows(rows):
        return [
            pl.BlockSpec((q_rows * rows, LANES), lambda i, w, p=p: (i, w[0] * parts + p))
            for p in range(parts)
        ]

    return pl.pallas_call(
        functools.partial(dress_a_kernel, parts),
        out_shape=[out] * chunks,
        grid_spec=pltpu.PrefetchScalarGridSpec(
            num_scalar_prefetch=1,
            grid=(shard // q_rows,),
            in_specs=windows(a_rows)
            + windows(occ_rows)
            + [pl.BlockSpec((a_rows * occ_rows, LANES), lambda i, w: (0, 0))],
            out_specs=[pl.BlockSpec((q_rows, out.shape[1]), lambda i, w: (i, 0))] * chunks,
        ),
        compiler_params=params(1),
        cost_estimate=pl.CostEstimate(
            flops=2 * shard * a_rows * occ_rows * c_tile,
            bytes_accessed=10 * shard * a_rows * c_tile,
            transcendentals=0,
        ),
    )(
        where,
        *[factor_a.reshape(shard * a_rows, wide)] * parts,
        *[factor_occ.reshape(shard * occ_rows, wide)] * parts,
        tables(singles_a),
    )


def dress_b_kernel(slots, where, *refs):
    pairs = slots // 2
    f_refs, occ_refs, tab_ref, outs = refs[:pairs], refs[pairs : 2 * pairs], refs[2 * pairs], refs[2 * pairs + 1 :]
    q_rows = outs[0].shape[0]
    b_rows = f_refs[0].shape[0] // q_rows
    occ_rows = occ_refs[0].shape[0] // q_rows
    lane = lax.broadcasted_iota(jnp.int32, (q_rows, LANES), 1)
    low_half = lane < LANES // 2
    even = lax.rem(lane // (LANES // GROUP), 2) == 0
    swap_slot = where[1] == 1
    swap_tile = where[2] == 1

    def roll(v, n):
        return pltpu.roll(v, n % LANES, 1)

    for pair in range(pairs):
        occ = [occ_refs[pair][pl.ds(k, q_rows, stride=occ_rows), :] for k in range(occ_rows)]

        def dressed(b):
            value = f_refs[pair][pl.ds(b, q_rows, stride=b_rows), :]
            for k in range(occ_rows):
                value = value - tab_ref[pl.ds(b * occ_rows + k, 1), :] * occ[k]
            return value

        for b in range(0, b_rows, GROUP):
            x0, x1, x2, x3 = (dressed(b + i) for i in range(GROUP))
            half = LANES // 2
            low0 = jnp.where(low_half, x0, roll(x2, half))
            high0 = jnp.where(low_half, roll(x0, half), x2)
            low1 = jnp.where(low_half, x1, roll(x3, half))
            high1 = jnp.where(low_half, roll(x1, half), x3)
            step = LANES // GROUP
            y00 = jnp.where(even, low0, roll(low1, step))
            y01 = jnp.where(even, roll(low0, -step), low1)
            y10 = jnp.where(even, high0, roll(high1, step))
            y11 = jnp.where(even, roll(high0, -step), high1)
            p00, p10 = jnp.where(swap_slot, y10, y00), jnp.where(swap_slot, y00, y10)
            p01, p11 = jnp.where(swap_slot, y11, y01), jnp.where(swap_slot, y01, y11)
            r00, r01 = jnp.where(swap_tile, p01, p00), jnp.where(swap_tile, p00, p01)
            r10, r11 = jnp.where(swap_tile, p11, p10), jnp.where(swap_tile, p10, p11)
            at = slice(b * step, b * step + LANES)
            outs[2 * pair][:, at] = r00.astype(BF16)
            outs[2 * pair + 1][:, at] = r10.astype(BF16)
            outs[slots + 2 * pair][:, at] = r01.astype(BF16)
            outs[slots + 2 * pair + 1][:, at] = r11.astype(BF16)


def dress_b(where, factor_b, factor_occ, singles_b, d_tile, slots):
    shard, b_rows, wide = factor_b.shape
    occ_rows = factor_occ.shape[1]
    q_rows = 16
    pairs = slots // 2
    out = jax.ShapeDtypeStruct((shard, b_rows * d_tile), BF16)

    def windows(rows):
        return [
            pl.BlockSpec((q_rows * rows, LANES), lambda i, w, p=p: (i, jnp.bitwise_xor(w[0], p)))
            for p in range(pairs)
        ]

    outs = pl.pallas_call(
        functools.partial(dress_b_kernel, slots),
        out_shape=[out] * (2 * slots),
        grid_spec=pltpu.PrefetchScalarGridSpec(
            num_scalar_prefetch=1,
            grid=(shard // q_rows,),
            in_specs=windows(b_rows)
            + windows(occ_rows)
            + [pl.BlockSpec((b_rows * occ_rows, LANES), lambda i, w: (0, 0))],
            out_specs=[pl.BlockSpec((q_rows, out.shape[1]), lambda i, w: (i, 0))] * (2 * slots),
        ),
        compiler_params=params(1),
        cost_estimate=pl.CostEstimate(
            flops=2 * shard * b_rows * occ_rows * wide,
            bytes_accessed=8 * shard * b_rows * wide,
            transcendentals=0,
        ),
    )(
        where,
        *[factor_b.reshape(shard * b_rows, wide)] * pairs,
        *[factor_occ.reshape(shard * occ_rows, wide)] * pairs,
        tables(singles_b),
    )
    return outs[:slots], outs[slots:]


def turn_kernel(slots, d_tile, *refs):
    blocks, o_ref, wide = refs[:slots], refs[slots], refs[slots + 1]
    columns = blocks[0].shape[1]
    for start in range(0, columns, LANES):
        tall = jnp.concatenate([r[:, start : start + LANES] for r in blocks], axis=0)
        flat = tall.astype(F32).T
        for part in range(wide.shape[0]):
            wide[part, start : start + LANES, :] = flat[:, part * LANES : (part + 1) * LANES]
    for d in range(d_tile):
        for part in range(wide.shape[0]):
            rows = wide[part, pl.ds(d, columns // d_tile, stride=d_tile), :]
            o_ref[d, :, part * LANES : (part + 1) * LANES] = rows.astype(BF16)


def turn(blocks, d_tile):
    slots = len(blocks)
    shard, columns = blocks[0].shape
    steps = columns // (16 * d_tile)
    depth = slots * shard
    return pl.pallas_call(
        functools.partial(turn_kernel, slots, d_tile),
        out_shape=jax.ShapeDtypeStruct((d_tile, columns // d_tile, depth), BF16),
        grid=(steps,),
        in_specs=[pl.BlockSpec((shard, columns // steps), lambda i: (0, i))] * slots,
        out_specs=pl.BlockSpec((d_tile, 16, depth), lambda i: (0, i, 0)),
        scratch_shapes=[pltpu.VMEM((depth // LANES, columns // steps, LANES), F32)],
        compiler_params=params(1),
        cost_estimate=pl.CostEstimate(
            flops=0, bytes_accessed=4 * depth * columns, transcendentals=0
        ),
    )(*blocks)


def ladder_kernel(slots, chunks, has_start, *refs):
    n = slots * chunks
    a_refs, (own_ref, other_ref, t_ref) = refs[:n], refs[n : n + 3]
    refs = refs[n + 3 :]
    starts, refs = (refs[:2], refs[2:]) if has_start else ((), refs)
    keep_ref, send_ref, whole_a, integral, total, sems = refs
    step = pl.program_id(0)
    shard, width = a_refs[0].shape

    def copies():
        return [
            pltpu.make_async_copy(
                a_refs[c * slots + k],
                whole_a.at[pl.ds(k * shard, shard), pl.ds(c * width, width)],
                sems.at[c * slots + k],
            )
            for c in range(chunks)
            for k in range(slots)
        ]

    half = total.shape[0] // 2

    @pl.when(step == 0)
    def _():
        for copy in copies():
            copy.start()
        if has_start:
            total[:half, :] = starts[0][...]
            total[half:, :] = starts[1][...]
        else:
            total[...] = jnp.zeros_like(total)
        for copy in copies():
            copy.wait()

    d_rows, b_local, depth = own_ref.shape
    c_tile = t_ref.shape[1]
    b_all = 2 * b_local
    rows = jnp.concatenate([own_ref[...], other_ref[...]], axis=1)
    rows = rows.reshape(d_rows * b_all, depth)
    for a in range(whole_a.shape[1] // c_tile):
        value = jnp.dot(
            rows, whole_a[:, a * c_tile : (a + 1) * c_tile], preferred_element_type=F32
        ).astype(BF16)
        for d in range(d_rows):
            integral[a * b_all : (a + 1) * b_all, d * c_tile : (d + 1) * c_tile] = value[
                d * b_all : (d + 1) * b_all
            ]
    weights = t_ref[...].reshape(d_rows * c_tile, t_ref.shape[2])
    total[...] += jnp.dot(integral[...], weights, preferred_element_type=F32)

    @pl.when(step == pl.num_programs(0) - 1)
    def _():
        keep_ref[...] = total[:half, :]
        send_ref[...] = total[half:, :]


def ladder(a_blocks, own, other, doubles, starts, d_rows=8):
    chunks, slots = len(a_blocks), len(a_blocks[0])
    shard, width = a_blocks[0][0].shape
    d_tile, b_local, depth = own.shape
    c_tile, pairs = doubles.shape[1:]
    columns = chunks * width
    a_rows = columns // c_tile
    rows = a_rows * 2 * b_local
    out = jax.ShapeDtypeStruct((rows // 2, pairs), F32)
    full = pl.BlockSpec((rows // 2, pairs), lambda i: (0, 0))
    return pl.pallas_call(
        functools.partial(ladder_kernel, slots, chunks, bool(starts)),
        out_shape=[out, out],
        grid=(d_tile // d_rows,),
        in_specs=[pl.BlockSpec(memory_space=pl.ANY)] * (chunks * slots)
        + [pl.BlockSpec((d_rows, b_local, depth), lambda i: (i, 0, 0))] * 2
        + [pl.BlockSpec((d_rows, c_tile, pairs), lambda i: (i, 0, 0))]
        + [full] * len(starts),
        out_specs=[full, full],
        scratch_shapes=[
            pltpu.VMEM((depth, columns), BF16),
            pltpu.VMEM((rows, d_rows * c_tile), BF16),
            pltpu.VMEM((rows, pairs), F32),
            pltpu.SemaphoreType.DMA((chunks * slots,)),
        ],
        compiler_params=params(1),
        cost_estimate=pl.CostEstimate(
            flops=2 * d_tile * 2 * b_local * columns * (depth + pairs),
            bytes_accessed=2 * depth * columns + 2 * doubles.size,
            transcendentals=0,
        ),
    )(*[b for chunk in a_blocks for b in chunk], own, other, doubles, *starts)


def exchange(value, bits, size):
    return lax.ppermute(value, "dev", [(d, d ^ bits) for d in range(size)])


def plane_gather(block, size, link):
    low, high = 2 * link, 4 * link

    def chain(d):
        return (d // low) % CHAIN

    middle = [(d, d ^ (low | high)) for d in range(size) if chain(d) in (1, 2)]
    outward = [(d, d ^ low) for d in range(size) if chain(d) in (1, 2)]
    position = chain(lax.axis_index("dev"))
    inner = (position == 1) | (position == 2)
    near = exchange(block, low, size)
    mid_own = lax.ppermute(block, "dev", middle)
    mid_near = lax.ppermute(near, "dev", middle)
    out_own = lax.ppermute(mid_own, "dev", outward)
    out_near = lax.ppermute(mid_near, "dev", outward)
    far = jnp.where(inner, mid_near, out_own)
    farthest = jnp.where(inner, mid_own, out_near)
    found = []
    for part in (block, near, far, farthest):
        found += [part, exchange(part, link, size)]
    return found


def fast_body(
    size,
    factor_a,
    factor_b,
    factor_occ,
    singles_a,
    singles_b,
    doubles,
    orbital_a,
    orbital_b,
    orbital_occ,
):
    c_tile, d_tile, pairs = doubles.shape
    a_rows, b_local = factor_a.shape[1], factor_b.shape[1]
    slots = size // 2
    chunks = 2
    col = lax.axis_index("col").astype(jnp.int32)
    dev = lax.axis_index("dev").astype(jnp.int32)
    tile, plane = dev % 2, dev // 2
    where_a = jnp.stack([col, col * (a_rows // 2)])
    where_b = jnp.stack([plane // 2, plane % 2, tile])

    blocks_a = dress_a(where_a, factor_a, factor_occ, singles_a, c_tile, chunks)
    mine = swap_doubles(doubles)
    theirs = exchange(mine, 1, size)
    halves = dress_b(where_b, factor_b, factor_occ, singles_b, d_tile, slots)
    whole_a = [plane_gather(block, size, 2) for block in blocks_a]
    partial_value = ()
    for half, weights in zip(halves, (mine, theirs)):
        found = [half[0]] + [exchange(half[k], 2 * k, size) for k in range(1, slots)]
        own = turn(found, d_tile)
        other = lax.ppermute(own, "col", [(0, 1), (1, 0)])
        partial_value = ladder(whole_a, own, other, weights, tuple(partial_value))
    keep, send = partial_value
    got = lax.ppermute(send, "col", [(0, 1), (1, 0)])
    a_half = a_rows // 2
    keep = keep.reshape(a_half, 2, b_local, pairs)
    got = got.reshape(a_half, 2, b_local, pairs)
    first = jnp.where(col == 0, keep[:, 0] + got[:, 1], keep[:, 1] + got[:, 0])
    second = jnp.where(col == 0, keep[:, 1] + got[:, 0], keep[:, 0] + got[:, 1])
    both = jnp.stack([first, second])
    b_own = 2 * b_local // size
    both = both.reshape(2, a_half, size // 2, b_own, pairs)
    both = jnp.transpose(both, (0, 2, 1, 3, 4)).reshape(size, a_half * b_own, pairs)
    moved = lax.all_to_all(both, "dev", split_axis=0, concat_axis=0, tiled=True)
    total = jnp.sum(moved, axis=0).reshape(a_half, b_own, pairs)
    pair_energy = (orbital_occ[:, None] + orbital_occ[None, :]).reshape(-1)
    denominator = orbital_a[:, None, None] + orbital_b[None, :, None] - pair_energy[None, None, :]
    return total / denominator


def plain_body(
    factor_a, factor_b, factor_occ, singles_a, singles_b, doubles, orbital_a, orbital_b, orbital_occ
):
    highest = lax.Precision.HIGHEST
    c_tile = doubles.shape[0]
    d_tile = doubles.shape[1]
    pair_count = doubles.shape[2]
    shard_rows = factor_a.shape[0]
    a_rows = factor_a.shape[1]
    b_local = factor_b.shape[1]
    d_groups = factor_b.shape[2] // d_tile
    col_index = lax.axis_index("col")
    occ_tile = lax.dynamic_slice_in_dim(factor_occ, col_index * c_tile, c_tile, 2)
    a_tile = lax.dynamic_slice_in_dim(factor_a, col_index * c_tile, c_tile, 2)
    dressed_a = (a_tile - jnp.einsum("ka,qkc->qac", singles_a, occ_tile, precision=highest)).astype(
        jnp.bfloat16
    )
    dressed_a = dressed_a.reshape(shard_rows, a_rows * c_tile)
    dressed_b = (
        factor_b - jnp.einsum("kb,qkd->qbd", singles_b, factor_occ, precision=highest)
    ).astype(jnp.bfloat16)
    grouped = dressed_b.reshape(shard_rows, b_local, d_groups, d_tile)
    grouped = jnp.transpose(grouped, (0, 2, 1, 3)).reshape(shard_rows, d_groups, b_local * d_tile)
    moved = lax.all_to_all(grouped, "dev", split_axis=1, concat_axis=0, tiled=True)
    collected = lax.all_gather(moved, "col", axis=1, tiled=True)
    whole_b = collected.reshape(collected.shape[0], -1)
    b_rows_all = whole_b.shape[1] // d_tile
    contract_first = (((0,), (0,)), ((), ()))
    whole_a = lax.all_gather(dressed_a, "dev", axis=0, tiled=True)
    integral = lax.dot_general(whole_a, whole_b, contract_first, preferred_element_type=jnp.float32)
    integral = integral.astype(jnp.bfloat16).reshape(a_rows, c_tile, b_rows_all, d_tile)
    integral = jnp.transpose(integral, (0, 2, 1, 3)).reshape(a_rows * b_rows_all, c_tile * d_tile)
    partial_value = jnp.dot(
        integral, doubles.reshape(c_tile * d_tile, pair_count), preferred_element_type=jnp.float32
    )
    partial_value = partial_value.reshape(a_rows, b_rows_all, pair_count)
    reduced = lax.psum_scatter(partial_value, "dev", scatter_dimension=1, tiled=True)
    total = lax.psum_scatter(reduced, "col", scatter_dimension=0, tiled=True)
    pair_energy = (orbital_occ[:, None] + orbital_occ[None, :]).reshape(-1)
    denominator = orbital_a[:, None, None] + orbital_b[None, :, None] - pair_energy[None, None, :]
    return total / denominator


def solution(mesh):
    size, columns = mesh.shape["dev"], mesh.shape["col"]

    def body(factor_a, factor_b, factor_occ, singles_a, singles_b, doubles, *orbitals):
        fits = (
            columns == 2
            and size == 4 * CHAIN
            and doubles.shape[1] * GROUP == LANES
            and doubles.shape[0] % LANES == 0
            and doubles.shape[2] % LANES == 0
            and factor_a.shape[0] % 16 == 0
            and factor_b.shape[1] % 16 == 0
        )
        chosen = functools.partial(fast_body, size) if fits else plain_body
        return chosen(factor_a, factor_b, factor_occ, singles_a, singles_b, doubles, *orbitals)

    return jax.shard_map(
        body,
        mesh=mesh,
        in_specs=(
            P("dev", None, None),
            P("dev", "col", None),
            P("dev", None, None),
            P(),
            P(None, "col"),
            P("col", "dev", None),
            P("col"),
            P("dev"),
            P(),
        ),
        out_specs=P("col", "dev", None),
        check_vma=False,
    )
```

```python
import functools

import jax
import jax.numpy as jnp
from jax import lax
from jax.experimental import pallas as pl
from jax.experimental.pallas import tpu as pltpu
from jax.sharding import PartitionSpec as P


F32 = jnp.float32
BF16 = jnp.bfloat16
LANES = 128
TALL = 16
GROUP = 4
CHAIN = 4


def params(n):
    return pltpu.CompilerParams(
        dimension_semantics=("arbitrary",) * n, vmem_limit_bytes=60 * 1024 * 1024
    )


def split(value, size):
    return jnp.right_shift(value, size.bit_length() - 1), jnp.bitwise_and(value, size - 1)


def reorder(inner, outer, shift=0):
    n = inner * outer
    row = lax.broadcasted_iota(jnp.int32, (n, 1), 0)
    column = lax.broadcasted_iota(jnp.int32, (1, n), 1)
    o, i = split(row, inner)
    source = i * outer + split(o + shift, outer)[1]
    return jnp.where(column == source, 1.0, 0.0).astype(BF16)


def halves_of(value):
    high = value.astype(BF16)
    return high, (value - high.astype(F32)).astype(BF16)


def spread(singles, q_rows):
    occ, rows = singles.shape
    exact = dict(precision=lax.Precision.HIGHEST, preferred_element_type=F32)
    high, wide = q_rows * rows, q_rows * occ
    row_q, row = split(lax.broadcasted_iota(jnp.int32, (high, 1), 0), rows)
    column_q, column = split(lax.broadcasted_iota(jnp.int32, (1, wide), 1), occ)
    pick_row = jnp.where(row == lax.broadcasted_iota(jnp.int32, (high, rows), 1), 1.0, 0.0)
    pick_k = jnp.where(column == lax.broadcasted_iota(jnp.int32, (occ, wide), 0), 1.0, 0.0)
    value = lax.dot_general(pick_row, singles, (((1,), (1,)), ((), ())), **exact)
    value = jnp.dot(value, pick_k, **exact)
    first, second = halves_of(jnp.where(row_q == column_q, value, 0.0))
    return jnp.concatenate([first, first, second], axis=1)


def dressed(factors, occ, mix_ref, order_ref):
    first, second = halves_of(occ)
    parts = jnp.concatenate([first, second, first], axis=0)
    change = jnp.dot(mix_ref[...], parts, preferred_element_type=F32)
    value = (factors - change).astype(BF16)
    return jnp.dot(order_ref[...], value, preferred_element_type=F32)


def swap_kernel(t_ref, o_ref, order):
    d_rows = t_ref.shape[1]

    @pl.when(pl.program_id(0) == 0)
    def _():
        order[...] = reorder(TALL, d_rows)

    for start in range(0, t_ref.shape[0], TALL):
        flat = t_ref[start : start + TALL].reshape(TALL * d_rows, t_ref.shape[2])
        value = jnp.dot(order[...], flat, preferred_element_type=F32).astype(BF16)
        for d in range(d_rows):
            o_ref[d, start : start + TALL, :] = value[d * TALL : (d + 1) * TALL]


def swap_doubles(doubles):
    c_tile, d_tile, pairs = doubles.shape
    rows = 4 * TALL
    return pl.pallas_call(
        swap_kernel,
        out_shape=jax.ShapeDtypeStruct((d_tile, c_tile, pairs), BF16),
        grid=(c_tile // rows,),
        in_specs=[pl.BlockSpec((rows, d_tile, pairs), lambda i: (i, 0, 0))],
        out_specs=pl.BlockSpec((d_tile, rows, pairs), lambda i: (0, i, 0)),
        scratch_shapes=[pltpu.VMEM((TALL * d_tile, TALL * d_tile), BF16)],
        compiler_params=params(1),
        cost_estimate=pl.CostEstimate(
            flops=0, bytes_accessed=4 * doubles.size, transcendentals=0
        ),
    )(doubles)


def dress_a_kernel(where, f_ref, occ_ref, singles_ref, out, mix, order):
    a_rows = f_ref.shape[0] // TALL
    width = f_ref.shape[1]

    @pl.when(pl.program_id(0) == 0)
    def _():
        mix[...] = spread(singles_ref[...], TALL)
        order[...] = reorder(TALL, a_rows, where[0] * (a_rows // 2))

    value = dressed(f_ref[...], occ_ref[...], mix, order).astype(BF16)
    for a in range(a_rows):
        out[:, a * width : (a + 1) * width] = value[a * TALL : (a + 1) * TALL]


def dress_a(col, factor_a, factor_occ, singles_a, c_tile):
    shard, a_rows, wide = factor_a.shape
    occ_rows = factor_occ.shape[1]
    columns = a_rows * c_tile
    return pl.pallas_call(
        dress_a_kernel,
        out_shape=jax.ShapeDtypeStruct((shard, columns), BF16),
        grid_spec=pltpu.PrefetchScalarGridSpec(
            num_scalar_prefetch=1,
            grid=(shard // TALL,),
            in_specs=[
                pl.BlockSpec((TALL * a_rows, c_tile), lambda i, w: (i, w[0])),
                pl.BlockSpec((TALL * occ_rows, c_tile), lambda i, w: (i, w[0])),
                pl.BlockSpec(singles_a.shape, lambda i, w: (0, 0)),
            ],
            out_specs=pl.BlockSpec((TALL, columns), lambda i, w: (i, 0)),
            scratch_shapes=[
                pltpu.VMEM((TALL * a_rows, 3 * TALL * occ_rows), BF16),
                pltpu.VMEM((TALL * a_rows, TALL * a_rows), BF16),
            ],
        ),
        compiler_params=params(1),
        cost_estimate=pl.CostEstimate(
            flops=2 * shard * a_rows * occ_rows * c_tile,
            bytes_accessed=10 * shard * a_rows * c_tile,
            transcendentals=0,
        ),
    )(
        col.reshape(1),
        factor_a.reshape(shard * a_rows, wide),
        factor_occ.reshape(shard * occ_rows, wide),
        singles_a,
    )


def dress_b_kernel(slots, where, *refs):
    pairs = slots // 2
    f_refs, occ_refs, singles_ref = refs[:pairs], refs[pairs : 2 * pairs], refs[2 * pairs]
    outs, (mix, order) = refs[2 * pairs + 1 : -2], refs[-2:]
    b_rows = f_refs[0].shape[0] // TALL

    @pl.when(pl.program_id(0) == 0)
    def _():
        mix[...] = spread(singles_ref[...], TALL)
        order[...] = reorder(TALL, b_rows)

    lane = lax.broadcasted_iota(jnp.int32, (TALL, LANES), 1)
    low_half = lane < LANES // 2
    even = jnp.bitwise_and(lane, LANES // GROUP) == 0
    swap_slot = lax.rem(where[0] // 2, 2) == 1
    swap_tile = lax.rem(where[0], 2) == 1

    def roll(v, n):
        return pltpu.roll(v, n % LANES, 1)

    both = dressed(
        jnp.concatenate([r[...] for r in f_refs], axis=1),
        jnp.concatenate([r[...] for r in occ_refs], axis=1),
        mix,
        order,
    )
    for pair in range(pairs):
        value = both[:, pair * LANES : (pair + 1) * LANES]
        for b in range(0, b_rows, GROUP):
            x0, x1, x2, x3 = (value[(b + i) * TALL : (b + i + 1) * TALL] for i in range(GROUP))
            half = LANES // 2
            low0 = jnp.where(low_half, x0, roll(x2, half))
            high0 = jnp.where(low_half, roll(x0, half), x2)
            low1 = jnp.where(low_half, x1, roll(x3, half))
            high1 = jnp.where(low_half, roll(x1, half), x3)
            step = LANES // GROUP
            y00 = jnp.where(even, low0, roll(low1, step))
            y01 = jnp.where(even, roll(low0, -step), low1)
            y10 = jnp.where(even, high0, roll(high1, step))
            y11 = jnp.where(even, roll(high0, -step), high1)
            p00, p10 = jnp.where(swap_slot, y10, y00), jnp.where(swap_slot, y00, y10)
            p01, p11 = jnp.where(swap_slot, y11, y01), jnp.where(swap_slot, y01, y11)
            r00, r01 = jnp.where(swap_tile, p01, p00), jnp.where(swap_tile, p00, p01)
            r10, r11 = jnp.where(swap_tile, p11, p10), jnp.where(swap_tile, p10, p11)
            at = slice(b * step, b * step + LANES)
            outs[2 * pair][:, at] = r00.astype(BF16)
            outs[2 * pair + 1][:, at] = r10.astype(BF16)
            outs[slots + 2 * pair][:, at] = r01.astype(BF16)
            outs[slots + 2 * pair + 1][:, at] = r11.astype(BF16)


def dress_b(dev, factor_b, factor_occ, singles_b, d_tile, slots):
    shard, b_rows, wide = factor_b.shape
    occ_rows = factor_occ.shape[1]
    pairs = slots // 2
    out = jax.ShapeDtypeStruct((shard, b_rows * d_tile), BF16)

    def windows(rows):
        return [
            pl.BlockSpec((TALL * rows, LANES), lambda i, w, p=p: (i, jnp.bitwise_xor(w[0] // 4, p)))
            for p in range(pairs)
        ]

    outs = pl.pallas_call(
        functools.partial(dress_b_kernel, slots),
        out_shape=[out] * (2 * slots),
        grid_spec=pltpu.PrefetchScalarGridSpec(
            num_scalar_prefetch=1,
            grid=(shard // TALL,),
            in_specs=windows(b_rows)
            + windows(occ_rows)
            + [pl.BlockSpec(singles_b.shape, lambda i, w: (0, 0))],
            out_specs=[pl.BlockSpec((TALL, out.shape[1]), lambda i, w: (i, 0))] * (2 * slots),
            scratch_shapes=[
                pltpu.VMEM((TALL * b_rows, 3 * TALL * occ_rows), BF16),
                pltpu.VMEM((TALL * b_rows, TALL * b_rows), BF16),
            ],
        ),
        compiler_params=params(1),
        cost_estimate=pl.CostEstimate(
            flops=2 * shard * b_rows * occ_rows * wide,
            bytes_accessed=8 * shard * b_rows * wide,
            transcendentals=0,
        ),
    )(
        dev.reshape(1),
        *[factor_b.reshape(shard * b_rows, wide)] * pairs,
        *[factor_occ.reshape(shard * occ_rows, wide)] * pairs,
        singles_b,
    )
    return outs[:slots], outs[slots:]


def turn_kernel(slots, d_tile, *refs):
    blocks, o_ref, order = refs[:slots], refs[slots], refs[slots + 1]

    @pl.when(pl.program_id(0) == 0)
    def _():
        order[...] = reorder(TALL, d_tile)

    tall = jnp.concatenate([r[...] for r in blocks], axis=0)
    value = lax.dot_general(
        order[...], tall, (((1,), (1,)), ((), ())), preferred_element_type=F32
    ).astype(BF16)
    for d in range(d_tile):
        o_ref[d] = value[d * TALL : (d + 1) * TALL]


def turn(blocks, d_tile):
    slots = len(blocks)
    shard, columns = blocks[0].shape
    width = TALL * d_tile
    depth = slots * shard
    return pl.pallas_call(
        functools.partial(turn_kernel, slots, d_tile),
        out_shape=jax.ShapeDtypeStruct((d_tile, columns // d_tile, depth), BF16),
        grid=(columns // width,),
        in_specs=[pl.BlockSpec((shard, width), lambda i: (0, i))] * slots,
        out_specs=pl.BlockSpec((d_tile, TALL, depth), lambda i: (0, i, 0)),
        scratch_shapes=[pltpu.VMEM((width, width), BF16)],
        compiler_params=params(1),
        cost_estimate=pl.CostEstimate(
            flops=0, bytes_accessed=4 * depth * columns, transcendentals=0
        ),
    )(*blocks)


def ladder_kernel(slots, chunks, has_start, *refs):
    n = slots * chunks
    a_refs, (own_ref, other_ref, t_ref) = refs[:n], refs[n : n + 3]
    refs = refs[n + 3 :]
    starts, refs = (refs[:2], refs[2:]) if has_start else ((), refs)
    keep_ref, send_ref, whole_a, integral, total, sems = refs
    step = pl.program_id(0)
    shard, width = a_refs[0].shape

    def copies():
        return [
            pltpu.make_async_copy(
                a_refs[c * slots + k],
                whole_a.at[pl.ds(k * shard, shard), pl.ds(c * width, width)],
                sems.at[c * slots + k],
            )
            for c in range(chunks)
            for k in range(slots)
        ]

    half = total.shape[0] // 2

    @pl.when(step == 0)
    def _():
        for copy in copies():
            copy.start()
        if has_start:
            total[:half, :] = starts[0][...]
            total[half:, :] = starts[1][...]
        else:
            total[...] = jnp.zeros_like(total)
        for copy in copies():
            copy.wait()

    d_rows, b_local, depth = own_ref.shape
    c_tile = t_ref.shape[1]
    b_all = 2 * b_local
    rows = jnp.concatenate([own_ref[...], other_ref[...]], axis=1)
    rows = rows.reshape(d_rows * b_all, depth)
    for a in range(whole_a.shape[1] // c_tile):
        value = jnp.dot(
            rows, whole_a[:, a * c_tile : (a + 1) * c_tile], preferred_element_type=F32
        ).astype(BF16)
        for d in range(d_rows):
            integral[a * b_all : (a + 1) * b_all, d * c_tile : (d + 1) * c_tile] = value[
                d * b_all : (d + 1) * b_all
            ]
    weights = t_ref[...].reshape(d_rows * c_tile, t_ref.shape[2])
    total[...] += jnp.dot(integral[...], weights, preferred_element_type=F32)

    @pl.when(step == pl.num_programs(0) - 1)
    def _():
        keep_ref[...] = total[:half, :]
        send_ref[...] = total[half:, :]


def ladder(a_blocks, own, other, doubles, starts, d_rows=8):
    chunks, slots = len(a_blocks), len(a_blocks[0])
    _, width = a_blocks[0][0].shape
    d_tile, b_local, depth = own.shape
    c_tile, pairs = doubles.shape[1:]
    columns = chunks * width
    a_rows = columns // c_tile
    rows = a_rows * 2 * b_local
    out = jax.ShapeDtypeStruct((rows // 2, pairs), F32)
    full = pl.BlockSpec((rows // 2, pairs), lambda i: (0, 0))
    return pl.pallas_call(
        functools.partial(ladder_kernel, slots, chunks, bool(starts)),
        out_shape=[out, out],
        grid=(d_tile // d_rows,),
        in_specs=[pl.BlockSpec(memory_space=pl.ANY)] * (chunks * slots)
        + [pl.BlockSpec((d_rows, b_local, depth), lambda i: (i, 0, 0))] * 2
        + [pl.BlockSpec((d_rows, c_tile, pairs), lambda i: (i, 0, 0))]
        + [full] * len(starts),
        out_specs=[full, full],
        scratch_shapes=[
            pltpu.VMEM((depth, columns), BF16),
            pltpu.VMEM((rows, d_rows * c_tile), BF16),
            pltpu.VMEM((rows, pairs), F32),
            pltpu.SemaphoreType.DMA((chunks * slots,)),
        ],
        compiler_params=params(1),
        cost_estimate=pl.CostEstimate(
            flops=2 * d_tile * 2 * b_local * columns * (depth + pairs),
            bytes_accessed=2 * depth * columns + 2 * doubles.size,
            transcendentals=0,
        ),
    )(*[b for chunk in a_blocks for b in chunk], own, other, doubles, *starts)


def exchange(value, bits, size):
    return lax.ppermute(value, "dev", [(d, d ^ bits) for d in range(size)])


def gated(value, *after):
    return lax.optimization_barrier((value,) + after)[0]


def plane_gather(block, size, link):
    low, high = 2 * link, 4 * link

    def chain(d):
        return (d // low) % CHAIN

    middle = [(d, d ^ (low | high)) for d in range(size) if chain(d) in (1, 2)]
    outward = [(d, d ^ low) for d in range(size) if chain(d) in (1, 2)]
    position = chain(lax.axis_index("dev"))
    inner = (position == 1) | (position == 2)
    near = exchange(block, low, size)
    mid_own = lax.ppermute(block, "dev", middle)
    mid_near = lax.ppermute(near, "dev", middle)
    out_own = lax.ppermute(mid_own, "dev", outward)
    out_near = lax.ppermute(mid_near, "dev", outward)
    far = jnp.where(inner, mid_near, out_own)
    farthest = jnp.where(inner, mid_own, out_near)
    found = []
    for part in (block, near, far, farthest):
        found += [part, exchange(part, link, size)]
    return found, (near, mid_near, out_own, far, farthest)


def fast_body(
    size,
    factor_a,
    factor_b,
    factor_occ,
    singles_a,
    singles_b,
    doubles,
    orbital_a,
    orbital_b,
    orbital_occ,
):
    c_tile, d_tile, pairs = doubles.shape
    a_rows, b_local = factor_a.shape[1], factor_b.shape[1]
    slots = size // 2
    col = lax.axis_index("col").astype(jnp.int32)
    dev = lax.axis_index("dev").astype(jnp.int32)
    block_a = dress_a(col, factor_a, factor_occ, singles_a, c_tile)
    mine = swap_doubles(doubles)
    theirs = exchange(mine, 1, size)
    whole_a, (near, mid_near, out_own, far, farthest) = plane_gather(block_a, size, 2)
    halves = dress_b(dev, factor_b, factor_occ, singles_b, d_tile, slots)
    partial_value = ()
    order = [slot for slot in (4, 6, 5, 7, 2, 3, 1) if slot < slots]
    for n, (half, weights) in enumerate(zip(halves, (mine, theirs))):
        found = {0: half[0]}
        for slot in order:
            if n:
                gate = farthest if slot in order[:2] else first[order[1]]
            else:
                gate = far if slot in order[:2] else farthest
            found[slot] = exchange(gated(half[slot], gate), 2 * slot, size)
        first = found
        own = turn([found[k] for k in range(slots)], d_tile)
        other = lax.ppermute(own, "col", [(0, 1), (1, 0)])
        partial_value = ladder([whole_a], own, other, weights, tuple(partial_value))
    keep, send = partial_value
    got = lax.ppermute(send, "col", [(0, 1), (1, 0)])
    a_half = a_rows // 2
    keep = keep.reshape(a_half, 2, b_local, pairs)
    got = got.reshape(a_half, 2, b_local, pairs)
    first = jnp.where(col == 0, keep[:, 0] + got[:, 1], keep[:, 1] + got[:, 0])
    second = jnp.where(col == 0, keep[:, 1] + got[:, 0], keep[:, 0] + got[:, 1])
    both = jnp.stack([first, second])
    b_own = 2 * b_local // size
    both = both.reshape(2, a_half, size // 2, b_own, pairs)
    both = jnp.transpose(both, (0, 2, 1, 3, 4)).reshape(size, a_half * b_own, pairs)
    moved = lax.all_to_all(both, "dev", split_axis=0, concat_axis=0, tiled=True)
    total = jnp.sum(moved, axis=0).reshape(a_half, b_own, pairs)
    pair_energy = (orbital_occ[:, None] + orbital_occ[None, :]).reshape(-1)
    denominator = orbital_a[:, None, None] + orbital_b[None, :, None] - pair_energy[None, None, :]
    return total / denominator


def plain_body(
    factor_a, factor_b, factor_occ, singles_a, singles_b, doubles, orbital_a, orbital_b, orbital_occ
):
    highest = lax.Precision.HIGHEST
    c_tile = doubles.shape[0]
    d_tile = doubles.shape[1]
    pair_count = doubles.shape[2]
    shard_rows = factor_a.shape[0]
    a_rows = factor_a.shape[1]
    b_local = factor_b.shape[1]
    d_groups = factor_b.shape[2] // d_tile
    col_index = lax.axis_index("col")
    occ_tile = lax.dynamic_slice_in_dim(factor_occ, col_index * c_tile, c_tile, 2)
    a_tile = lax.dynamic_slice_in_dim(factor_a, col_index * c_tile, c_tile, 2)
    dressed_a = (a_tile - jnp.einsum("ka,qkc->qac", singles_a, occ_tile, precision=highest)).astype(
        jnp.bfloat16
    )
    dressed_a = dressed_a.reshape(shard_rows, a_rows * c_tile)
    dressed_b = (
        factor_b - jnp.einsum("kb,qkd->qbd", singles_b, factor_occ, precision=highest)
    ).astype(jnp.bfloat16)
    grouped = dressed_b.reshape(shard_rows, b_local, d_groups, d_tile)
    grouped = jnp.transpose(grouped, (0, 2, 1, 3)).reshape(shard_rows, d_groups, b_local * d_tile)
    moved = lax.all_to_all(grouped, "dev", split_axis=1, concat_axis=0, tiled=True)
    collected = lax.all_gather(moved, "col", axis=1, tiled=True)
    whole_b = collected.reshape(collected.shape[0], -1)
    b_rows_all = whole_b.shape[1] // d_tile
    contract_first = (((0,), (0,)), ((), ()))
    whole_a = lax.all_gather(dressed_a, "dev", axis=0, tiled=True)
    integral = lax.dot_general(whole_a, whole_b, contract_first, preferred_element_type=jnp.float32)
    integral = integral.astype(jnp.bfloat16).reshape(a_rows, c_tile, b_rows_all, d_tile)
    integral = jnp.transpose(integral, (0, 2, 1, 3)).reshape(a_rows * b_rows_all, c_tile * d_tile)
    partial_value = jnp.dot(
        integral, doubles.reshape(c_tile * d_tile, pair_count), preferred_element_type=jnp.float32
    )
    partial_value = partial_value.reshape(a_rows, b_rows_all, pair_count)
    reduced = lax.psum_scatter(partial_value, "dev", scatter_dimension=1, tiled=True)
    total = lax.psum_scatter(reduced, "col", scatter_dimension=0, tiled=True)
    pair_energy = (orbital_occ[:, None] + orbital_occ[None, :]).reshape(-1)
    denominator = orbital_a[:, None, None] + orbital_b[None, :, None] - pair_energy[None, None, :]
    return total / denominator


def solution(mesh):
    size, columns = mesh.shape["dev"], mesh.shape["col"]

    def body(factor_a, factor_b, factor_occ, singles_a, singles_b, doubles, *orbitals):
        fits = (
            columns == 2
            and size == 4 * CHAIN
            and doubles.shape[1] * GROUP == LANES
            and doubles.shape[0] % LANES == 0
            and doubles.shape[2] % LANES == 0
            and factor_a.shape[0] % TALL == 0
            and factor_b.shape[1] % TALL == 0
        )
        chosen = functools.partial(fast_body, size) if fits else plain_body
        return chosen(factor_a, factor_b, factor_occ, singles_a, singles_b, doubles, *orbitals)

    return jax.shard_map(
        body,
        mesh=mesh,
        in_specs=(
            P("dev", None, None),
            P("dev", "col", None),
            P("dev", None, None),
            P(),
            P(None, "col"),
            P("col", "dev", None),
            P("col"),
            P("dev"),
            P(),
        ),
        out_specs=P("col", "dev", None),
        check_vma=False,
    )
```

```python
import functools

import jax
import jax.numpy as jnp
from jax import lax
from jax.experimental import pallas as pl
from jax.experimental.pallas import tpu as pltpu
from jax.sharding import PartitionSpec as P


F32 = jnp.float32
BF16 = jnp.bfloat16
LANES = 128
TALL = 16
GROUP = 4
CHAIN = 4


def params(n):
    return pltpu.CompilerParams(
        dimension_semantics=("arbitrary",) * n, vmem_limit_bytes=60 * 1024 * 1024
    )


def split(value, size):
    return jnp.right_shift(value, size.bit_length() - 1), jnp.bitwise_and(value, size - 1)


def reorder(inner, outer, shift=0):
    n = inner * outer
    row = lax.broadcasted_iota(jnp.int32, (n, 1), 0)
    column = lax.broadcasted_iota(jnp.int32, (1, n), 1)
    o, i = split(row, inner)
    source = i * outer + split(o + shift, outer)[1]
    return jnp.where(column == source, 1.0, 0.0).astype(BF16)


def halves_of(value):
    high = value.astype(BF16)
    return high, (value - high.astype(F32)).astype(BF16)


def spread(singles, q_rows):
    occ, rows = singles.shape
    exact = dict(precision=lax.Precision.HIGHEST, preferred_element_type=F32)
    high, wide = q_rows * rows, q_rows * occ
    row_q, row = split(lax.broadcasted_iota(jnp.int32, (high, 1), 0), rows)
    column_q, column = split(lax.broadcasted_iota(jnp.int32, (1, wide), 1), occ)
    pick_row = jnp.where(row == lax.broadcasted_iota(jnp.int32, (high, rows), 1), 1.0, 0.0)
    pick_k = jnp.where(column == lax.broadcasted_iota(jnp.int32, (occ, wide), 0), 1.0, 0.0)
    value = lax.dot_general(pick_row, singles, (((1,), (1,)), ((), ())), **exact)
    value = jnp.dot(value, pick_k, **exact)
    first, second = halves_of(jnp.where(row_q == column_q, value, 0.0))
    return jnp.concatenate([first, first, second], axis=1)


def dressed(factors, occ, mix_ref, order_ref):
    first, second = halves_of(occ)
    parts = jnp.concatenate([first, second, first], axis=0)
    change = jnp.dot(mix_ref[...], parts, preferred_element_type=F32)
    value = (factors - change).astype(BF16)
    return jnp.dot(order_ref[...], value, preferred_element_type=F32)


def swap_kernel(t_ref, o_ref, order):
    d_rows = t_ref.shape[1]

    @pl.when(pl.program_id(0) == 0)
    def _():
        order[...] = reorder(TALL, d_rows)

    for start in range(0, t_ref.shape[0], TALL):
        flat = t_ref[start : start + TALL].reshape(TALL * d_rows, t_ref.shape[2])
        value = jnp.dot(order[...], flat, preferred_element_type=F32).astype(BF16)
        for d in range(d_rows):
            o_ref[d, start : start + TALL, :] = value[d * TALL : (d + 1) * TALL]


def swap_doubles(doubles):
    c_tile, d_tile, pairs = doubles.shape
    rows = 4 * TALL
    return pl.pallas_call(
        swap_kernel,
        out_shape=jax.ShapeDtypeStruct((d_tile, c_tile, pairs), BF16),
        grid=(c_tile // rows,),
        in_specs=[pl.BlockSpec((rows, d_tile, pairs), lambda i: (i, 0, 0))],
        out_specs=pl.BlockSpec((d_tile, rows, pairs), lambda i: (0, i, 0)),
        scratch_shapes=[pltpu.VMEM((TALL * d_tile, TALL * d_tile), BF16)],
        compiler_params=params(1),
        cost_estimate=pl.CostEstimate(
            flops=0, bytes_accessed=4 * doubles.size, transcendentals=0
        ),
    )(doubles)


def dress_a_kernel(where, f_ref, occ_ref, singles_ref, first, second, mix, order):
    a_rows = f_ref.shape[0] // TALL
    width = f_ref.shape[1]

    @pl.when(pl.program_id(0) == 0)
    def _():
        mix[...] = spread(singles_ref[...], TALL)
        order[...] = reorder(TALL, a_rows, where[0] * (a_rows // 2))

    value = dressed(f_ref[...], occ_ref[...], mix, order).astype(BF16)
    half = a_rows // 2
    for a in range(half):
        at = slice(a * width, (a + 1) * width)
        first[:, at] = value[a * TALL : (a + 1) * TALL]
        second[:, at] = value[(half + a) * TALL : (half + a + 1) * TALL]


def dress_a(col, factor_a, factor_occ, singles_a, c_tile):
    shard, a_rows, wide = factor_a.shape
    occ_rows = factor_occ.shape[1]
    columns = a_rows // 2 * c_tile
    return pl.pallas_call(
        dress_a_kernel,
        out_shape=[jax.ShapeDtypeStruct((shard, columns), BF16)] * 2,
        grid_spec=pltpu.PrefetchScalarGridSpec(
            num_scalar_prefetch=1,
            grid=(shard // TALL,),
            in_specs=[
                pl.BlockSpec((TALL * a_rows, c_tile), lambda i, w: (i, w[0])),
                pl.BlockSpec((TALL * occ_rows, c_tile), lambda i, w: (i, w[0])),
                pl.BlockSpec(singles_a.shape, lambda i, w: (0, 0)),
            ],
            out_specs=[pl.BlockSpec((TALL, columns), lambda i, w: (i, 0))] * 2,
            scratch_shapes=[
                pltpu.VMEM((TALL * a_rows, 3 * TALL * occ_rows), BF16),
                pltpu.VMEM((TALL * a_rows, TALL * a_rows), BF16),
            ],
        ),
        compiler_params=params(1),
        cost_estimate=pl.CostEstimate(
            flops=2 * shard * a_rows * occ_rows * c_tile,
            bytes_accessed=10 * shard * a_rows * c_tile,
            transcendentals=0,
        ),
    )(
        col.reshape(1),
        factor_a.reshape(shard * a_rows, wide),
        factor_occ.reshape(shard * occ_rows, wide),
        singles_a,
    )


def dress_b_kernel(slots, where, *refs):
    pairs = slots // 2
    f_refs, occ_refs, singles_ref = refs[:pairs], refs[pairs : 2 * pairs], refs[2 * pairs]
    outs, (mix, order) = refs[2 * pairs + 1 : -2], refs[-2:]
    b_rows = f_refs[0].shape[0] // TALL

    @pl.when(pl.program_id(0) == 0)
    def _():
        mix[...] = spread(singles_ref[...], TALL)
        order[...] = reorder(TALL, b_rows)

    lane = lax.broadcasted_iota(jnp.int32, (TALL, LANES), 1)
    low_half = lane < LANES // 2
    even = jnp.bitwise_and(lane, LANES // GROUP) == 0
    swap_slot = lax.rem(where[0] // 2, 2) == 1
    swap_tile = lax.rem(where[0], 2) == 1

    def roll(v, n):
        return pltpu.roll(v, n % LANES, 1)

    both = dressed(
        jnp.concatenate([r[...] for r in f_refs], axis=1),
        jnp.concatenate([r[...] for r in occ_refs], axis=1),
        mix,
        order,
    )
    for pair in range(pairs):
        value = both[:, pair * LANES : (pair + 1) * LANES]
        for b in range(0, b_rows, GROUP):
            x0, x1, x2, x3 = (value[(b + i) * TALL : (b + i + 1) * TALL] for i in range(GROUP))
            half = LANES // 2
            low0 = jnp.where(low_half, x0, roll(x2, half))
            high0 = jnp.where(low_half, roll(x0, half), x2)
            low1 = jnp.where(low_half, x1, roll(x3, half))
            high1 = jnp.where(low_half, roll(x1, half), x3)
            step = LANES // GROUP
            y00 = jnp.where(even, low0, roll(low1, step))
            y01 = jnp.where(even, roll(low0, -step), low1)
            y10 = jnp.where(even, high0, roll(high1, step))
            y11 = jnp.where(even, roll(high0, -step), high1)
            p00, p10 = jnp.where(swap_slot, y10, y00), jnp.where(swap_slot, y00, y10)
            p01, p11 = jnp.where(swap_slot, y11, y01), jnp.where(swap_slot, y01, y11)
            r00, r01 = jnp.where(swap_tile, p01, p00), jnp.where(swap_tile, p00, p01)
            r10, r11 = jnp.where(swap_tile, p11, p10), jnp.where(swap_tile, p10, p11)
            at = slice(b * step, b * step + LANES)
            outs[2 * pair][:, at] = r00.astype(BF16)
            outs[2 * pair + 1][:, at] = r10.astype(BF16)
            outs[slots + 2 * pair][:, at] = r01.astype(BF16)
            outs[slots + 2 * pair + 1][:, at] = r11.astype(BF16)


def dress_b(dev, factor_b, factor_occ, singles_b, d_tile, slots):
    shard, b_rows, wide = factor_b.shape
    occ_rows = factor_occ.shape[1]
    pairs = slots // 2
    out = jax.ShapeDtypeStruct((shard, b_rows * d_tile), BF16)

    def windows(rows):
        return [
            pl.BlockSpec((TALL * rows, LANES), lambda i, w, p=p: (i, jnp.bitwise_xor(w[0] // 4, p)))
            for p in range(pairs)
        ]

    outs = pl.pallas_call(
        functools.partial(dress_b_kernel, slots),
        out_shape=[out] * (2 * slots),
        grid_spec=pltpu.PrefetchScalarGridSpec(
            num_scalar_prefetch=1,
            grid=(shard // TALL,),
            in_specs=windows(b_rows)
            + windows(occ_rows)
            + [pl.BlockSpec(singles_b.shape, lambda i, w: (0, 0))],
            out_specs=[pl.BlockSpec((TALL, out.shape[1]), lambda i, w: (i, 0))] * (2 * slots),
            scratch_shapes=[
                pltpu.VMEM((TALL * b_rows, 3 * TALL * occ_rows), BF16),
                pltpu.VMEM((TALL * b_rows, TALL * b_rows), BF16),
            ],
        ),
        compiler_params=params(1),
        cost_estimate=pl.CostEstimate(
            flops=2 * shard * b_rows * occ_rows * wide,
            bytes_accessed=8 * shard * b_rows * wide,
            transcendentals=0,
        ),
    )(
        dev.reshape(1),
        *[factor_b.reshape(shard * b_rows, wide)] * pairs,
        *[factor_occ.reshape(shard * occ_rows, wide)] * pairs,
        singles_b,
    )
    return outs[:slots], outs[slots:]


def turn_kernel(slots, d_tile, *refs):
    blocks, o_ref, order = refs[:slots], refs[slots], refs[slots + 1]

    @pl.when(pl.program_id(0) == 0)
    def _():
        order[...] = reorder(TALL, d_tile)

    tall = jnp.concatenate([r[...] for r in blocks], axis=0)
    value = lax.dot_general(
        order[...], tall, (((1,), (1,)), ((), ())), preferred_element_type=F32
    ).astype(BF16)
    for d in range(d_tile):
        o_ref[d] = value[d * TALL : (d + 1) * TALL]


def turn(blocks, d_tile):
    slots = len(blocks)
    shard, columns = blocks[0].shape
    width = TALL * d_tile
    depth = slots * shard
    return pl.pallas_call(
        functools.partial(turn_kernel, slots, d_tile),
        out_shape=jax.ShapeDtypeStruct((d_tile, columns // d_tile, depth), BF16),
        grid=(columns // width,),
        in_specs=[pl.BlockSpec((shard, width), lambda i: (0, i))] * slots,
        out_specs=pl.BlockSpec((d_tile, TALL, depth), lambda i: (0, i, 0)),
        scratch_shapes=[pltpu.VMEM((width, width), BF16)],
        compiler_params=params(1),
        cost_estimate=pl.CostEstimate(
            flops=0, bytes_accessed=4 * depth * columns, transcendentals=0
        ),
    )(*blocks)


def ladder_kernel(slots, chunks, has_start, own_rows, *refs):
    n = slots * chunks
    a_refs, (own_ref, other_ref, t_ref) = refs[:n], refs[n : n + 3]
    refs = refs[n + 3 :]
    starts, refs = (refs[:chunks], refs[chunks:]) if has_start else ((), refs)
    outs, (whole_a, integral, total, sems) = refs[:chunks], refs[chunks:]
    step = pl.program_id(0)
    shard, width = a_refs[0].shape

    def copies():
        return [
            pltpu.make_async_copy(
                a_refs[c * slots + k],
                whole_a.at[pl.ds(k * shard, shard), pl.ds(c * width, width)],
                sems.at[c * slots + k],
            )
            for c in range(chunks)
            for k in range(slots)
        ]

    part = total.shape[0] // chunks

    @pl.when(step == 0)
    def _():
        for copy in copies():
            copy.start()
        if has_start:
            for n in range(chunks):
                total[n * part : (n + 1) * part, :] = starts[n][...]
        else:
            total[...] = jnp.zeros_like(total)
        for copy in copies():
            copy.wait()

    d_rows, b_local, depth = own_ref.shape
    c_tile = t_ref.shape[1]
    b_all = 2 * b_local
    rows = jnp.concatenate([own_ref[...], other_ref[...]], axis=1)
    rows = rows.reshape(d_rows * b_all, depth)
    for a in range(whole_a.shape[1] // c_tile):
        value = jnp.dot(
            rows, whole_a[:, a * c_tile : (a + 1) * c_tile], preferred_element_type=F32
        ).astype(BF16)
        for d in range(d_rows):
            integral[a * b_all : (a + 1) * b_all, d * c_tile : (d + 1) * c_tile] = value[
                d * b_all : (d + 1) * b_all
            ]
    weights = t_ref[...].reshape(d_rows * c_tile, t_ref.shape[2])
    total[...] += jnp.dot(integral[...], weights, preferred_element_type=F32)

    @pl.when(step == pl.num_programs(0) - 1)
    def _():
        for n, out in enumerate(outs):
            if own_rows is None:
                out[...] = total[n * part : (n + 1) * part, :]
                continue
            for a in range(part // b_all):
                for b in range(0, b_all, own_rows):
                    source = n * part + a * b_all + b
                    side, owner = divmod(b, b_local)
                    out[side, owner // own_rows, a * own_rows : (a + 1) * own_rows, :] = total[
                        source : source + own_rows, :
                    ]


def ladder(a_blocks, own, other, doubles, starts, own_rows=None, d_rows=8):
    chunks, slots = len(a_blocks), len(a_blocks[0])
    _, width = a_blocks[0][0].shape
    d_tile, b_local, depth = own.shape
    c_tile, pairs = doubles.shape[1:]
    columns = chunks * width
    a_rows = columns // c_tile
    rows = a_rows * 2 * b_local
    full = pl.BlockSpec((rows // chunks, pairs), lambda i: (0, 0))
    if own_rows is None:
        out, out_spec = jax.ShapeDtypeStruct((rows // chunks, pairs), F32), full
    else:
        shape = (2, b_local // own_rows, a_rows // chunks * own_rows, pairs)
        out, out_spec = jax.ShapeDtypeStruct(shape, F32), pl.BlockSpec(shape, lambda i: (0,) * 4)
    return pl.pallas_call(
        functools.partial(ladder_kernel, slots, chunks, bool(starts), own_rows),
        out_shape=[out] * chunks,
        grid=(d_tile // d_rows,),
        in_specs=[pl.BlockSpec(memory_space=pl.ANY)] * (chunks * slots)
        + [pl.BlockSpec((d_rows, b_local, depth), lambda i: (i, 0, 0))] * 2
        + [pl.BlockSpec((d_rows, c_tile, pairs), lambda i: (i, 0, 0))]
        + [full] * len(starts),
        out_specs=[out_spec] * chunks,
        scratch_shapes=[
            pltpu.VMEM((depth, columns), BF16),
            pltpu.VMEM((rows, d_rows * c_tile), BF16),
            pltpu.VMEM((rows, pairs), F32),
            pltpu.SemaphoreType.DMA((chunks * slots,)),
        ],
        compiler_params=params(1),
        cost_estimate=pl.CostEstimate(
            flops=2 * d_tile * 2 * b_local * columns * (depth + pairs),
            bytes_accessed=2 * depth * columns + 2 * doubles.size,
            transcendentals=0,
        ),
    )(*[b for chunk in a_blocks for b in chunk], own, other, doubles, *starts)


def exchange(value, bits, size):
    return lax.ppermute(value, "dev", [(d, d ^ bits) for d in range(size)])


def gated(value, *after):
    return lax.optimization_barrier((value,) + after)[0]


def plane_gather(block, size, link):
    low, high = 2 * link, 4 * link

    def chain(d):
        return (d // low) % CHAIN

    middle = [(d, d ^ (low | high)) for d in range(size) if chain(d) in (1, 2)]
    outward = [(d, d ^ low) for d in range(size) if chain(d) in (1, 2)]
    position = chain(lax.axis_index("dev"))
    inner = (position == 1) | (position == 2)
    near = exchange(block, low, size)
    mid_own = lax.ppermute(block, "dev", middle)
    mid_near = lax.ppermute(near, "dev", middle)
    out_own = lax.ppermute(mid_own, "dev", outward)
    out_near = lax.ppermute(mid_near, "dev", outward)
    far = jnp.where(inner, mid_near, out_own)
    farthest = jnp.where(inner, mid_own, out_near)
    found = []
    for part in (block, near, far, farthest):
        found += [part, exchange(part, link, size)]
    return found, dict(near=near, far=far, farthest=farthest)


def fast_body(
    size,
    factor_a,
    factor_b,
    factor_occ,
    singles_a,
    singles_b,
    doubles,
    orbital_a,
    orbital_b,
    orbital_occ,
):
    c_tile, d_tile, pairs = doubles.shape
    a_rows, b_local = factor_a.shape[1], factor_b.shape[1]
    slots = size // 2
    b_own = 2 * b_local // size
    col = lax.axis_index("col").astype(jnp.int32)
    dev = lax.axis_index("dev").astype(jnp.int32)
    blocks_a = dress_a(col, factor_a, factor_occ, singles_a, c_tile)
    mine = swap_doubles(doubles)
    theirs = exchange(mine, 1, size)
    whole0, marks0 = plane_gather(blocks_a[0], size, 2)
    whole1, marks1 = plane_gather(gated(blocks_a[1], marks0["near"]), size, 2)
    halves = dress_b(dev, factor_b, factor_occ, singles_b, d_tile, slots)
    order = [slot for slot in (4, 6, 2, 5, 7, 3, 1) if slot < slots]
    sides = []
    for n, half in enumerate(halves):
        found = {0: half[0]}
        for slot in order:
            gate = marks1["farthest"] if n else marks0["far"]
            found[slot] = exchange(gated(half[slot], gate), 2 * slot, size)
        own = turn([found[k] for k in range(slots)], d_tile)
        other = lax.ppermute(own, "col", [(0, 1), (1, 0)])
        sides.append((own, other))
    (keep,) = ladder([whole0], *sides[0], mine, (), d_rows=4)
    (send,) = ladder([whole1], *sides[0], mine, (), d_rows=4)
    keep, send = ladder([whole0, whole1], *sides[1], theirs, (keep, send), b_own)
    got = lax.ppermute(send, "col", [(0, 1), (1, 0)])
    near, far = keep[0] + got[1], keep[1] + got[0]
    both = jnp.where(col == 0, jnp.stack([near, far]), jnp.stack([far, near]))
    a_half = a_rows // 2
    both = both.astype(BF16).reshape(size, a_half * b_own, pairs)
    moved = lax.all_to_all(both, "dev", split_axis=0, concat_axis=0, tiled=True)
    total = jnp.sum(moved.astype(F32), axis=0).reshape(a_half, b_own, pairs)
    pair_energy = (orbital_occ[:, None] + orbital_occ[None, :]).reshape(-1)
    denominator = orbital_a[:, None, None] + orbital_b[None, :, None] - pair_energy[None, None, :]
    return total / denominator


def plain_body(
    factor_a, factor_b, factor_occ, singles_a, singles_b, doubles, orbital_a, orbital_b, orbital_occ
):
    highest = lax.Precision.HIGHEST
    c_tile = doubles.shape[0]
    d_tile = doubles.shape[1]
    pair_count = doubles.shape[2]
    shard_rows = factor_a.shape[0]
    a_rows = factor_a.shape[1]
    b_local = factor_b.shape[1]
    d_groups = factor_b.shape[2] // d_tile
    col_index = lax.axis_index("col")
    occ_tile = lax.dynamic_slice_in_dim(factor_occ, col_index * c_tile, c_tile, 2)
    a_tile = lax.dynamic_slice_in_dim(factor_a, col_index * c_tile, c_tile, 2)
    dressed_a = (a_tile - jnp.einsum("ka,qkc->qac", singles_a, occ_tile, precision=highest)).astype(
        jnp.bfloat16
    )
    dressed_a = dressed_a.reshape(shard_rows, a_rows * c_tile)
    dressed_b = (
        factor_b - jnp.einsum("kb,qkd->qbd", singles_b, factor_occ, precision=highest)
    ).astype(jnp.bfloat16)
    grouped = dressed_b.reshape(shard_rows, b_local, d_groups, d_tile)
    grouped = jnp.transpose(grouped, (0, 2, 1, 3)).reshape(shard_rows, d_groups, b_local * d_tile)
    moved = lax.all_to_all(grouped, "dev", split_axis=1, concat_axis=0, tiled=True)
    collected = lax.all_gather(moved, "col", axis=1, tiled=True)
    whole_b = collected.reshape(collected.shape[0], -1)
    b_rows_all = whole_b.shape[1] // d_tile
    contract_first = (((0,), (0,)), ((), ()))
    whole_a = lax.all_gather(dressed_a, "dev", axis=0, tiled=True)
    integral = lax.dot_general(whole_a, whole_b, contract_first, preferred_element_type=jnp.float32)
    integral = integral.astype(jnp.bfloat16).reshape(a_rows, c_tile, b_rows_all, d_tile)
    integral = jnp.transpose(integral, (0, 2, 1, 3)).reshape(a_rows * b_rows_all, c_tile * d_tile)
    partial_value = jnp.dot(
        integral, doubles.reshape(c_tile * d_tile, pair_count), preferred_element_type=jnp.float32
    )
    partial_value = partial_value.reshape(a_rows, b_rows_all, pair_count)
    reduced = lax.psum_scatter(partial_value, "dev", scatter_dimension=1, tiled=True)
    total = lax.psum_scatter(reduced, "col", scatter_dimension=0, tiled=True)
    pair_energy = (orbital_occ[:, None] + orbital_occ[None, :]).reshape(-1)
    denominator = orbital_a[:, None, None] + orbital_b[None, :, None] - pair_energy[None, None, :]
    return total / denominator


def solution(mesh):
    size, columns = mesh.shape["dev"], mesh.shape["col"]

    def body(factor_a, factor_b, factor_occ, singles_a, singles_b, doubles, *orbitals):
        fits = (
            columns == 2
            and size == 4 * CHAIN
            and doubles.shape[1] * GROUP == LANES
            and doubles.shape[0] % LANES == 0
            and doubles.shape[2] % LANES == 0
            and factor_a.shape[0] % TALL == 0
            and factor_b.shape[1] % TALL == 0
        )
        chosen = functools.partial(fast_body, size) if fits else plain_body
        return chosen(factor_a, factor_b, factor_occ, singles_a, singles_b, doubles, *orbitals)

    return jax.shard_map(
        body,
        mesh=mesh,
        in_specs=(
            P("dev", None, None),
            P("dev", "col", None),
            P("dev", None, None),
            P(),
            P(None, "col"),
            P("col", "dev", None),
            P("col"),
            P("dev"),
            P(),
        ),
        out_specs=P("col", "dev", None),
        check_vma=False,
    )
```

```python
import functools

import jax
import jax.numpy as jnp
from jax import lax
from jax.experimental import pallas as pl
from jax.experimental.pallas import tpu as pltpu
from jax.sharding import PartitionSpec as P


F32 = jnp.float32
BF16 = jnp.bfloat16
LANES = 128
TALL = 16
GROUP = 4
CHAIN = 4


def params(mebibytes):
    return pltpu.CompilerParams(
        dimension_semantics=("arbitrary",), vmem_limit_bytes=mebibytes * 1024 * 1024
    )


def split(value, size):
    return jnp.right_shift(value, size.bit_length() - 1), jnp.bitwise_and(value, size - 1)


def reorder(inner, outer, shift=0):
    n = inner * outer
    row = lax.broadcasted_iota(jnp.int32, (n, 1), 0)
    column = lax.broadcasted_iota(jnp.int32, (1, n), 1)
    o, i = split(row, inner)
    source = i * outer + split(o + shift, outer)[1]
    return jnp.where(column == source, 1.0, 0.0).astype(BF16)


def halves_of(value):
    high = value.astype(BF16)
    return high, (value - high.astype(F32)).astype(BF16)


def spread(singles, q_rows):
    occ, rows = singles.shape
    exact = dict(precision=lax.Precision.HIGHEST, preferred_element_type=F32)
    high, wide = q_rows * rows, q_rows * occ
    row_q, row = split(lax.broadcasted_iota(jnp.int32, (high, 1), 0), rows)
    column_q, column = split(lax.broadcasted_iota(jnp.int32, (1, wide), 1), occ)
    pick_row = jnp.where(row == lax.broadcasted_iota(jnp.int32, (high, rows), 1), 1.0, 0.0)
    pick_k = jnp.where(column == lax.broadcasted_iota(jnp.int32, (occ, wide), 0), 1.0, 0.0)
    value = lax.dot_general(pick_row, singles, (((1,), (1,)), ((), ())), **exact)
    value = jnp.dot(value, pick_k, **exact)
    first, second = halves_of(jnp.where(row_q == column_q, value, 0.0))
    return jnp.concatenate([first, first, second], axis=1)


def dressed(factors, occ, mix_ref, order_ref):
    first, second = halves_of(occ)
    parts = jnp.concatenate([first, second, first], axis=0)
    change = jnp.dot(mix_ref[...], parts, preferred_element_type=F32)
    value = (factors - change).astype(BF16)
    return jnp.dot(order_ref[...], value, preferred_element_type=F32)


def swap_kernel(t_ref, o_ref, order):
    d_rows = t_ref.shape[1]

    @pl.when(pl.program_id(0) == 0)
    def _():
        order[...] = reorder(TALL, d_rows)

    for start in range(0, t_ref.shape[0], TALL):
        flat = t_ref[start : start + TALL].reshape(TALL * d_rows, t_ref.shape[2])
        value = jnp.dot(order[...], flat, preferred_element_type=F32).astype(BF16)
        for d in range(d_rows):
            o_ref[d, start : start + TALL, :] = value[d * TALL : (d + 1) * TALL]


def swap_doubles(doubles):
    c_tile, d_tile, pairs = doubles.shape
    rows = 4 * TALL
    return pl.pallas_call(
        swap_kernel,
        out_shape=jax.ShapeDtypeStruct((d_tile, c_tile, pairs), BF16),
        grid=(c_tile // rows,),
        in_specs=[pl.BlockSpec((rows, d_tile, pairs), lambda i: (i, 0, 0))],
        out_specs=pl.BlockSpec((d_tile, rows, pairs), lambda i: (0, i, 0)),
        scratch_shapes=[pltpu.VMEM((TALL * d_tile, TALL * d_tile), BF16)],
        compiler_params=params(16),
        cost_estimate=pl.CostEstimate(
            flops=0, bytes_accessed=4 * doubles.size, transcendentals=0
        ),
    )(doubles)


def dress_a_kernel(where, f_ref, occ_ref, singles_ref, first, second, mix, order):
    a_rows = f_ref.shape[0] // TALL
    width = f_ref.shape[1]

    @pl.when(pl.program_id(0) == 0)
    def _():
        mix[...] = spread(singles_ref[...], TALL)
        order[...] = reorder(TALL, a_rows, where[0] * (a_rows // 2))

    value = dressed(f_ref[...], occ_ref[...], mix, order).astype(BF16)
    half = a_rows // 2
    for a in range(half):
        at = slice(a * width, (a + 1) * width)
        first[:, at] = value[a * TALL : (a + 1) * TALL]
        second[:, at] = value[(half + a) * TALL : (half + a + 1) * TALL]


def dress_a(col, factor_a, factor_occ, singles_a, c_tile):
    shard, a_rows, wide = factor_a.shape
    occ_rows = factor_occ.shape[1]
    columns = a_rows // 2 * c_tile
    return pl.pallas_call(
        dress_a_kernel,
        out_shape=[jax.ShapeDtypeStruct((shard, columns), BF16)] * 2,
        grid_spec=pltpu.PrefetchScalarGridSpec(
            num_scalar_prefetch=1,
            grid=(shard // TALL,),
            in_specs=[
                pl.BlockSpec((TALL * a_rows, c_tile), lambda i, w: (i, w[0])),
                pl.BlockSpec((TALL * occ_rows, c_tile), lambda i, w: (i, w[0])),
                pl.BlockSpec(singles_a.shape, lambda i, w: (0, 0)),
            ],
            out_specs=[pl.BlockSpec((TALL, columns), lambda i, w: (i, 0))] * 2,
            scratch_shapes=[
                pltpu.VMEM((TALL * a_rows, 3 * TALL * occ_rows), BF16),
                pltpu.VMEM((TALL * a_rows, TALL * a_rows), BF16),
            ],
        ),
        compiler_params=params(60),
        cost_estimate=pl.CostEstimate(
            flops=2 * shard * a_rows * occ_rows * c_tile,
            bytes_accessed=10 * shard * a_rows * c_tile,
            transcendentals=0,
        ),
    )(
        col.reshape(1),
        factor_a.reshape(shard * a_rows, wide),
        factor_occ.reshape(shard * occ_rows, wide),
        singles_a,
    )


def dress_b_kernel(slots, where, *refs):
    pairs = slots // 2
    f_refs, occ_refs, singles_ref = refs[:pairs], refs[pairs : 2 * pairs], refs[2 * pairs]
    outs, (mix, order) = refs[2 * pairs + 1 : -2], refs[-2:]
    b_rows = f_refs[0].shape[0] // TALL

    @pl.when(pl.program_id(0) == 0)
    def _():
        mix[...] = spread(singles_ref[...], TALL)
        order[...] = reorder(TALL, b_rows)

    lane = lax.broadcasted_iota(jnp.int32, (TALL, LANES), 1)
    low_half = lane < LANES // 2
    even = jnp.bitwise_and(lane, LANES // GROUP) == 0
    swap_slot = lax.rem(where[0] // 2, 2) == 1
    swap_tile = lax.rem(where[0], 2) == 1

    def roll(v, n):
        return pltpu.roll(v, n % LANES, 1)

    both = dressed(
        jnp.concatenate([r[...] for r in f_refs], axis=1),
        jnp.concatenate([r[...] for r in occ_refs], axis=1),
        mix,
        order,
    )
    for pair in range(pairs):
        value = both[:, pair * LANES : (pair + 1) * LANES]
        for b in range(0, b_rows, GROUP):
            x0, x1, x2, x3 = (value[(b + i) * TALL : (b + i + 1) * TALL] for i in range(GROUP))
            half = LANES // 2
            low0 = jnp.where(low_half, x0, roll(x2, half))
            high0 = jnp.where(low_half, roll(x0, half), x2)
            low1 = jnp.where(low_half, x1, roll(x3, half))
            high1 = jnp.where(low_half, roll(x1, half), x3)
            step = LANES // GROUP
            y00 = jnp.where(even, low0, roll(low1, step))
            y01 = jnp.where(even, roll(low0, -step), low1)
            y10 = jnp.where(even, high0, roll(high1, step))
            y11 = jnp.where(even, roll(high0, -step), high1)
            p00, p10 = jnp.where(swap_slot, y10, y00), jnp.where(swap_slot, y00, y10)
            p01, p11 = jnp.where(swap_slot, y11, y01), jnp.where(swap_slot, y01, y11)
            r00, r01 = jnp.where(swap_tile, p01, p00), jnp.where(swap_tile, p00, p01)
            r10, r11 = jnp.where(swap_tile, p11, p10), jnp.where(swap_tile, p10, p11)
            at = slice(b * step, b * step + LANES)
            outs[2 * pair][:, at] = r00.astype(BF16)
            outs[2 * pair + 1][:, at] = r10.astype(BF16)
            outs[slots + 2 * pair][:, at] = r01.astype(BF16)
            outs[slots + 2 * pair + 1][:, at] = r11.astype(BF16)


def dress_b(dev, factor_b, factor_occ, singles_b, d_tile, slots):
    shard, b_rows, wide = factor_b.shape
    occ_rows = factor_occ.shape[1]
    pairs = slots // 2
    out = jax.ShapeDtypeStruct((shard, b_rows * d_tile), BF16)

    def windows(rows):
        return [
            pl.BlockSpec((TALL * rows, LANES), lambda i, w, p=p: (i, jnp.bitwise_xor(w[0] // 4, p)))
            for p in range(pairs)
        ]

    outs = pl.pallas_call(
        functools.partial(dress_b_kernel, slots),
        out_shape=[out] * (2 * slots),
        grid_spec=pltpu.PrefetchScalarGridSpec(
            num_scalar_prefetch=1,
            grid=(shard // TALL,),
            in_specs=windows(b_rows)
            + windows(occ_rows)
            + [pl.BlockSpec(singles_b.shape, lambda i, w: (0, 0))],
            out_specs=[pl.BlockSpec((TALL, out.shape[1]), lambda i, w: (i, 0))] * (2 * slots),
            scratch_shapes=[
                pltpu.VMEM((TALL * b_rows, 3 * TALL * occ_rows), BF16),
                pltpu.VMEM((TALL * b_rows, TALL * b_rows), BF16),
            ],
        ),
        compiler_params=params(56),
        cost_estimate=pl.CostEstimate(
            flops=2 * shard * b_rows * occ_rows * wide,
            bytes_accessed=8 * shard * b_rows * wide,
            transcendentals=0,
        ),
    )(
        dev.reshape(1),
        *[factor_b.reshape(shard * b_rows, wide)] * pairs,
        *[factor_occ.reshape(shard * occ_rows, wide)] * pairs,
        singles_b,
    )
    return outs[:slots], outs[slots:]


def turn_kernel(slots, d_tile, *refs):
    blocks, o_ref, order = refs[:slots], refs[slots], refs[slots + 1]

    @pl.when(pl.program_id(0) == 0)
    def _():
        order[...] = reorder(TALL, d_tile)

    tall = jnp.concatenate([r[...] for r in blocks], axis=0)
    value = lax.dot_general(
        order[...], tall, (((1,), (1,)), ((), ())), preferred_element_type=F32
    ).astype(BF16)
    for d in range(d_tile):
        o_ref[d] = value[d * TALL : (d + 1) * TALL]


def turn(blocks, d_tile):
    slots = len(blocks)
    shard, columns = blocks[0].shape
    width = TALL * d_tile
    depth = slots * shard
    return pl.pallas_call(
        functools.partial(turn_kernel, slots, d_tile),
        out_shape=jax.ShapeDtypeStruct((d_tile, columns // d_tile, depth), BF16),
        grid=(columns // width,),
        in_specs=[pl.BlockSpec((shard, width), lambda i: (0, i))] * slots,
        out_specs=pl.BlockSpec((d_tile, TALL, depth), lambda i: (0, i, 0)),
        scratch_shapes=[pltpu.VMEM((width, width), BF16)],
        compiler_params=params(16),
        cost_estimate=pl.CostEstimate(
            flops=0, bytes_accessed=4 * depth * columns, transcendentals=0
        ),
    )(*blocks)


def ladder_kernel(slots, chunks, has_start, own_rows, *refs):
    n = slots * chunks
    a_refs, (own_ref, other_ref, t_ref) = refs[:n], refs[n : n + 3]
    refs = refs[n + 3 :]
    starts, refs = (refs[:chunks], refs[chunks:]) if has_start else ((), refs)
    outs, (whole_a, integral, total, sems) = refs[:chunks], refs[chunks:]
    step = pl.program_id(0)
    shard, width = a_refs[0].shape

    def copies():
        return [
            pltpu.make_async_copy(
                a_refs[c * slots + k],
                whole_a.at[pl.ds(k * shard, shard), pl.ds(c * width, width)],
                sems.at[c * slots + k],
            )
            for c in range(chunks)
            for k in range(slots)
        ]

    part = total.shape[0] // chunks

    @pl.when(step == 0)
    def _():
        for copy in copies():
            copy.start()
        if has_start:
            for n in range(chunks):
                total[n * part : (n + 1) * part, :] = starts[n][...]
        else:
            total[...] = jnp.zeros_like(total)
        for copy in copies():
            copy.wait()

    d_rows, b_local, depth = own_ref.shape
    c_tile = t_ref.shape[1]
    b_all = 2 * b_local
    rows = jnp.concatenate([own_ref[...], other_ref[...]], axis=1)
    rows = rows.reshape(d_rows * b_all, depth)
    for a in range(whole_a.shape[1] // c_tile):
        value = jnp.dot(
            rows, whole_a[:, a * c_tile : (a + 1) * c_tile], preferred_element_type=F32
        ).astype(BF16)
        for d in range(d_rows):
            integral[a * b_all : (a + 1) * b_all, d * c_tile : (d + 1) * c_tile] = value[
                d * b_all : (d + 1) * b_all
            ]
    weights = t_ref[...].reshape(d_rows * c_tile, t_ref.shape[2])
    total[...] += jnp.dot(integral[...], weights, preferred_element_type=F32)

    @pl.when(step == pl.num_programs(0) - 1)
    def _():
        for n, out in enumerate(outs):
            if own_rows is None:
                out[...] = total[n * part : (n + 1) * part, :]
                continue
            for a in range(part // b_all):
                for b in range(0, b_all, own_rows):
                    source = n * part + a * b_all + b
                    side, owner = divmod(b, b_local)
                    out[side, owner // own_rows, a * own_rows : (a + 1) * own_rows, :] = total[
                        source : source + own_rows, :
                    ]


def ladder(a_blocks, own, other, doubles, starts, own_rows=None, d_rows=8):
    chunks, slots = len(a_blocks), len(a_blocks[0])
    _, width = a_blocks[0][0].shape
    d_tile, b_local, depth = own.shape
    c_tile, pairs = doubles.shape[1:]
    columns = chunks * width
    a_rows = columns // c_tile
    rows = a_rows * 2 * b_local
    full = pl.BlockSpec((rows // chunks, pairs), lambda i: (0, 0))
    if own_rows is None:
        out, out_spec = jax.ShapeDtypeStruct((rows // chunks, pairs), F32), full
    else:
        shape = (2, b_local // own_rows, a_rows // chunks * own_rows, pairs)
        out, out_spec = jax.ShapeDtypeStruct(shape, F32), pl.BlockSpec(shape, lambda i: (0,) * 4)
    return pl.pallas_call(
        functools.partial(ladder_kernel, slots, chunks, bool(starts), own_rows),
        out_shape=[out] * chunks,
        grid=(d_tile // d_rows,),
        in_specs=[pl.BlockSpec(memory_space=pl.ANY)] * (chunks * slots)
        + [pl.BlockSpec((d_rows, b_local, depth), lambda i: (i, 0, 0))] * 2
        + [pl.BlockSpec((d_rows, c_tile, pairs), lambda i: (i, 0, 0))]
        + [full] * len(starts),
        out_specs=[out_spec] * chunks,
        scratch_shapes=[
            pltpu.VMEM((depth, columns), BF16),
            pltpu.VMEM((rows, d_rows * c_tile), BF16),
            pltpu.VMEM((rows, pairs), F32),
            pltpu.SemaphoreType.DMA((chunks * slots,)),
        ],
        compiler_params=params(28),
        cost_estimate=pl.CostEstimate(
            flops=2 * d_tile * 2 * b_local * columns * (depth + pairs),
            bytes_accessed=2 * depth * columns + 2 * doubles.size,
            transcendentals=0,
        ),
    )(*[b for chunk in a_blocks for b in chunk], own, other, doubles, *starts)


def exchange(value, bits, size):
    return lax.ppermute(value, "dev", [(d, d ^ bits) for d in range(size)])


def gated(value, *after):
    return lax.optimization_barrier((value,) + after)[0]


def plane_gather(block, size, link):
    low, high = 2 * link, 4 * link

    def chain(d):
        return (d // low) % CHAIN

    middle = [(d, d ^ (low | high)) for d in range(size) if chain(d) in (1, 2)]
    outward = [(d, d ^ low) for d in range(size) if chain(d) in (1, 2)]
    position = chain(lax.axis_index("dev"))
    inner = (position == 1) | (position == 2)
    near = exchange(block, low, size)
    mid_own = lax.ppermute(block, "dev", middle)
    mid_near = lax.ppermute(near, "dev", middle)
    out_own = lax.ppermute(mid_own, "dev", outward)
    out_near = lax.ppermute(mid_near, "dev", outward)
    far = jnp.where(inner, mid_near, out_own)
    farthest = jnp.where(inner, mid_own, out_near)
    found = []
    for part in (block, near, far, farthest):
        found += [part, exchange(part, link, size)]
    return found, dict(near=near, far=far, farthest=farthest)


def fast_body(
    size,
    factor_a,
    factor_b,
    factor_occ,
    singles_a,
    singles_b,
    doubles,
    orbital_a,
    orbital_b,
    orbital_occ,
):
    c_tile, d_tile, pairs = doubles.shape
    a_rows, b_local = factor_a.shape[1], factor_b.shape[1]
    slots = size // 2
    b_own = 2 * b_local // size
    col = lax.axis_index("col").astype(jnp.int32)
    dev = lax.axis_index("dev").astype(jnp.int32)
    blocks_a = dress_a(col, factor_a, factor_occ, singles_a, c_tile)
    mine = swap_doubles(doubles)
    theirs = exchange(mine, 1, size)
    whole0, marks0 = plane_gather(blocks_a[0], size, 2)
    whole1, marks1 = plane_gather(gated(blocks_a[1], marks0["near"]), size, 2)
    halves = dress_b(dev, factor_b, factor_occ, singles_b, d_tile, slots)
    order = [slot for slot in (4, 6, 2, 5, 7, 3, 1) if slot < slots]
    sides = []
    for n, half in enumerate(halves):
        found = {0: half[0]}
        for slot in order:
            gate = marks1["farthest"] if n else marks0["far" if slot == 1 else "farthest"]
            found[slot] = exchange(gated(half[slot], gate), 2 * slot, size)
        own = turn([found[k] for k in range(slots)], d_tile)
        other = lax.ppermute(own, "col", [(0, 1), (1, 0)])
        sides.append((own, other))
    (keep,) = ladder([whole0], *sides[0], mine, (), d_rows=4)
    (send,) = ladder([whole1], *sides[0], mine, (), d_rows=4)
    keep, send = ladder([whole0, whole1], *sides[1], theirs, (keep, send), b_own)
    got = lax.ppermute(send, "col", [(0, 1), (1, 0)])
    near, far = keep[0] + got[1], keep[1] + got[0]
    both = jnp.where(col == 0, jnp.stack([near, far]), jnp.stack([far, near]))
    a_half = a_rows // 2
    both = both.astype(BF16).reshape(size, a_half * b_own, pairs)
    moved = lax.all_to_all(both, "dev", split_axis=0, concat_axis=0, tiled=True)
    total = jnp.sum(moved.astype(F32), axis=0).reshape(a_half, b_own, pairs)
    pair_energy = (orbital_occ[:, None] + orbital_occ[None, :]).reshape(-1)
    denominator = orbital_a[:, None, None] + orbital_b[None, :, None] - pair_energy[None, None, :]
    return total / denominator


def plain_body(
    factor_a, factor_b, factor_occ, singles_a, singles_b, doubles, orbital_a, orbital_b, orbital_occ
):
    highest = lax.Precision.HIGHEST
    c_tile = doubles.shape[0]
    d_tile = doubles.shape[1]
    pair_count = doubles.shape[2]
    shard_rows = factor_a.shape[0]
    a_rows = factor_a.shape[1]
    b_local = factor_b.shape[1]
    d_groups = factor_b.shape[2] // d_tile
    col_index = lax.axis_index("col")
    occ_tile = lax.dynamic_slice_in_dim(factor_occ, col_index * c_tile, c_tile, 2)
    a_tile = lax.dynamic_slice_in_dim(factor_a, col_index * c_tile, c_tile, 2)
    dressed_a = (a_tile - jnp.einsum("ka,qkc->qac", singles_a, occ_tile, precision=highest)).astype(
        jnp.bfloat16
    )
    dressed_a = dressed_a.reshape(shard_rows, a_rows * c_tile)
    dressed_b = (
        factor_b - jnp.einsum("kb,qkd->qbd", singles_b, factor_occ, precision=highest)
    ).astype(jnp.bfloat16)
    grouped = dressed_b.reshape(shard_rows, b_local, d_groups, d_tile)
    grouped = jnp.transpose(grouped, (0, 2, 1, 3)).reshape(shard_rows, d_groups, b_local * d_tile)
    moved = lax.all_to_all(grouped, "dev", split_axis=1, concat_axis=0, tiled=True)
    collected = lax.all_gather(moved, "col", axis=1, tiled=True)
    whole_b = collected.reshape(collected.shape[0], -1)
    b_rows_all = whole_b.shape[1] // d_tile
    contract_first = (((0,), (0,)), ((), ()))
    whole_a = lax.all_gather(dressed_a, "dev", axis=0, tiled=True)
    integral = lax.dot_general(whole_a, whole_b, contract_first, preferred_element_type=jnp.float32)
    integral = integral.astype(jnp.bfloat16).reshape(a_rows, c_tile, b_rows_all, d_tile)
    integral = jnp.transpose(integral, (0, 2, 1, 3)).reshape(a_rows * b_rows_all, c_tile * d_tile)
    partial_value = jnp.dot(
        integral, doubles.reshape(c_tile * d_tile, pair_count), preferred_element_type=jnp.float32
    )
    partial_value = partial_value.reshape(a_rows, b_rows_all, pair_count)
    reduced = lax.psum_scatter(partial_value, "dev", scatter_dimension=1, tiled=True)
    total = lax.psum_scatter(reduced, "col", scatter_dimension=0, tiled=True)
    pair_energy = (orbital_occ[:, None] + orbital_occ[None, :]).reshape(-1)
    denominator = orbital_a[:, None, None] + orbital_b[None, :, None] - pair_energy[None, None, :]
    return total / denominator


def solution(mesh):
    size, columns = mesh.shape["dev"], mesh.shape["col"]

    def body(factor_a, factor_b, factor_occ, singles_a, singles_b, doubles, *orbitals):
        fits = (
            columns == 2
            and size == 4 * CHAIN
            and doubles.shape[1] * GROUP == LANES
            and doubles.shape[0] % LANES == 0
            and doubles.shape[2] % LANES == 0
            and factor_a.shape[0] % TALL == 0
            and factor_b.shape[1] % TALL == 0
        )
        chosen = functools.partial(fast_body, size) if fits else plain_body
        return chosen(factor_a, factor_b, factor_occ, singles_a, singles_b, doubles, *orbitals)

    return jax.shard_map(
        body,
        mesh=mesh,
        in_specs=(
            P("dev", None, None),
            P("dev", "col", None),
            P("dev", None, None),
            P(),
            P(None, "col"),
            P("col", "dev", None),
            P("col"),
            P("dev"),
            P(),
        ),
        out_specs=P("col", "dev", None),
        check_vma=False,
    )
```
